128 devices in a mesh: rep: 4 (over y), ep: 32 (over z, x, core).
Axes of the slice: x: 4, y: 4, z: 4, core: 2. Of those that a mesh axis runs over, the one named last changes fastest.
Arguments:
- tokens: bfloat16 [16384, 4096], P(('rep', 'ep')), may hold values from -6 to 6
- routes: int32 [16384, 8], P(('rep', 'ep')), may hold values from 0 to 31, as said below
- gate_scores: float32 [16384, 8], P(('rep', 'ep')), may hold values from 0.1 to 1
- slot_order: int32 [128, 128], P(('rep', 'ep')), may hold values from 0 to 127, each once within a row
- capacity: int32 [4, 32], replicated, may hold values from 384 to 1536, as said below
- w_gate: bfloat16 [32, 4096, 768], P('ep'), may hold values from -0.09375 to 0.09375
- w_up: bfloat16 [32, 4096, 768], P('ep'), may hold values from -0.09375 to 0.09375
- w_down: bfloat16 [32, 768, 4096], P('ep'), may hold values from -0.21875 to 0.21875
Outputs:
- mixed: bfloat16 [16384, 4096], P(('rep', 'ep'))
The draws below stay inside these ranges and needn't reach their ends.
Inputs may be any that keep to these rules, and one draw needn't show every extreme that they name: `routes`: each row names 8 different experts; among the rows of one device no expert is named more than 40 times, and some device names some expert exactly 40 times. `slot_order`: each device's row is a permutation; a smaller value is served earlier. `capacity`: some entry equals 1536 and some equals 384.
All inputs are finite; a program needn't handle non-finite values.
Results may differ from the reference program's by a relative error of at most 0.0058.
Values may be sent and summed in bfloat16 or wider, within the bound.
A program may use at most 192 MiB of HBM per device.

```python
import math
import jax
import jax.numpy as jnp
from jax import lax

D = 4096
FF = 768
TOP = 8
TOK_DEV = 128
EXPERTS = 32
TOKENS = 16384
SLOT = 40
CAP = 1536
SPILL = 768
N_REP = 4
N_EP = 32
DEVICES = 128


def draw_capacity(key, part):
    floor_value = CAP // 4
    entries = N_REP * EXPERTS
    values = jax.random.randint(key, (entries,), floor_value, CAP + 1)
    first = jax.random.randint(jax.random.fold_in(key, 11), (), 0, entries)
    other = jax.random.randint(jax.random.fold_in(key, 12), (), 0, entries - 1)
    second = (first + 1 + other) % entries
    values = values.at[first].set(CAP).at[second].set(floor_value)
    return values.reshape(N_REP, EXPERTS).astype(jnp.int32)


def draw_routes(key, part):
    window_least = (4 * EXPERTS + 4) // 5
    perm_keys = jax.random.split(jax.random.fold_in(key, 21), N_REP)
    group_perm = jax.vmap(lambda single: jax.random.permutation(single, EXPERTS))(perm_keys).astype(jnp.int32)
    widths = jax.random.randint(jax.random.fold_in(key, 22), (N_REP,), window_least, EXPERTS + 1)
    widths = widths.at[0].set(window_least).astype(jnp.int32)
    shifts = jax.random.randint(jax.random.fold_in(key, 23), (N_REP, N_EP), 0, EXPERTS).astype(jnp.int32)
    places = jnp.arange(TOK_DEV * TOP, dtype=jnp.int32).reshape(TOK_DEV, TOP)
    window_pos = (shifts[:, :, None, None] + places[None, None, :, :]) % widths[:, None, None, None]
    group_ids = jnp.arange(N_REP, dtype=jnp.int32)[:, None, None, None]
    chosen = group_perm[group_ids, window_pos]
    return chosen.reshape(TOKENS, TOP).astype(jnp.int32)


def levels(rng, dims, cuts, least, high):
    def one(position, blocks):
        heights = jax.random.uniform(jax.random.fold_in(jax.random.fold_in(rng, 6), position), (blocks,), jnp.float32, least / len(cuts), high / len(cuts))
        return jnp.repeat(jnp.exp(heights), dims[position] // blocks).reshape((-1,) + (1,) * (len(dims) - position - 1))

    gain = one(*cuts[0])
    for cut in cuts[1:]:
        gain = gain * one(*cut)
    return gain


def normal_values(stream_key, extent, deviation, bound, pieces=(), held_as=jnp.bfloat16):
    gain = levels(stream_key, extent, pieces, -0.22, 0.18) if pieces else 1.0
    values = jax.random.normal(stream_key, extent, jnp.float32) * deviation * gain
    return jnp.minimum(jnp.maximum(values, -bound), bound).astype(held_as)


def setup_inputs(seed: int = 0) -> dict:
    splits = jax.random.split(jax.random.key(seed), 9)
    return {
        "tokens": normal_values(splits[0], (TOKENS, D), 1.0, 6.0, ((0, 128),)),
        "routes": draw_routes(jax.random.fold_in(splits[8], 71), 0),
        "gate_scores": jnp.clip(jnp.exp(math.log(1.0) - 2.3025851 * jax.random.uniform(splits[2], (TOKENS, TOP), jnp.float32) ** levels(splits[2], (TOKENS, TOP), ((0, 128),), -0.2, 0.2)), 0.1, 1.0),
        "slot_order": jax.vmap(lambda own: jax.random.permutation(own, TOK_DEV))(jax.random.split(splits[3], DEVICES)).reshape((DEVICES, TOK_DEV)).astype(jnp.int32),
        "capacity": draw_capacity(jax.random.fold_in(splits[8], 71), 0),
        "w_gate": normal_values(splits[5], (EXPERTS, D, FF), D ** -0.5, 0.09375, ((0, 32),)),
        "w_up": normal_values(splits[6], (EXPERTS, D, FF), D ** -0.5, 0.09375, ((0, 32),)),
        "w_down": normal_values(splits[7], (EXPERTS, FF, D), FF ** -0.5, 0.21875, ((0, 32),)),
    }


def expert_rows(inputs, w_gate, w_up, w_down):
    gate_proj = jnp.dot(inputs, w_gate, preferred_element_type=jnp.float32)
    up_proj = jnp.dot(inputs, w_up, preferred_element_type=jnp.float32)
    hidden = (jax.nn.silu(gate_proj) * up_proj).astype(jnp.bfloat16)
    return jnp.dot(hidden, w_down, preferred_element_type=jnp.float32).astype(jnp.bfloat16)


def reference(tokens, routes, gate_scores, slot_order, capacity, w_gate, w_up, w_down):
    groups = N_REP
    blocks = N_EP
    features = tokens.reshape(groups, blocks, TOK_DEV, D)
    picks = routes.reshape(groups, blocks, TOK_DEV, TOP)
    scores = gate_scores.reshape(groups, blocks, TOK_DEV, TOP).astype(jnp.float32)
    priority = slot_order.reshape(groups, blocks, TOK_DEV)
    expert_ids = jnp.arange(EXPERTS, dtype=jnp.int32)
    onehot = (picks[..., None] == expert_ids).astype(jnp.float32)
    hit = jnp.sum(onehot, axis=3)
    before = (priority[..., None, :] < priority[..., :, None]).astype(jnp.float32)
    rank = jnp.einsum("gsab,gsbe->gsae", before, hit, precision=lax.Precision.HIGHEST)
    counts = jnp.sum(hit, axis=2)
    start = jnp.cumsum(counts, axis=1) - counts
    load = jnp.sum(counts, axis=1)
    cap_values = capacity.astype(jnp.float32)
    partner = jnp.bitwise_xor(jnp.arange(groups, dtype=jnp.int32), 1) % groups
    spare = jnp.minimum(jnp.maximum(cap_values[partner] - load[partner], 0.0), float(SPILL))
    limit_row = cap_values + spare
    kept_hit = hit * ((start[:, :, None, :] + rank) < limit_row[:, None, None, :]).astype(jnp.float32)
    kept_mask = jnp.sum(onehot * kept_hit[..., None, :], axis=4)
    gate_total = jnp.sum(scores, axis=3)
    kept_sum = jnp.sum(scores * kept_mask, axis=3)
    weight = scores * kept_mask / jnp.maximum(kept_sum, 0.25 * gate_total)[..., None]
    slot_ids = jnp.arange(SLOT, dtype=jnp.float32)
    token_ids = jnp.arange(TOK_DEV, dtype=jnp.float32)

    def one_expert(mixed_sum, expert_pack):
        expert, gate_w, up_w, down_w = expert_pack
        hit_e = jnp.take(hit, expert, axis=3)
        rank_e = jnp.take(rank, expert, axis=3)
        slot_match = hit_e[..., None] * (rank_e[..., None] == slot_ids).astype(jnp.float32)
        source_tok = jnp.sum(slot_match * token_ids[:, None], axis=2).astype(jnp.int32)
        rows_e = jnp.take_along_axis(features, source_tok[..., None], axis=2)
        outputs = expert_rows(rows_e.reshape(-1, D), gate_w, up_w, down_w).reshape(groups, blocks, SLOT, D)
        rank_int = jnp.clip(rank_e.astype(jnp.int32), 0, SLOT - 1)
        taken = jnp.take_along_axis(outputs, rank_int[..., None], axis=2)
        weight_e = jnp.sum(weight * jnp.take(onehot, expert, axis=4), axis=3)
        return mixed_sum + weight_e[..., None] * taken.astype(jnp.float32), None

    initial = jnp.zeros((groups, blocks, TOK_DEV, D), jnp.float32)
    mixed_sum, _ = lax.scan(one_expert, initial, (expert_ids, w_gate, w_up, w_down))
    return mixed_sum.reshape(TOKENS, D).astype(jnp.bfloat16)
```

```python
import jax
import jax.numpy as jnp
from jax import lax
from jax.sharding import PartitionSpec as P

SLOT = 40
SPILL = 768.0


def routing(routes, slot_order, capacity):
    experts = lax.axis_size("ep")
    groups = lax.axis_size("rep")
    ep_index = lax.axis_index("ep")
    rep_index = lax.axis_index("rep")
    expert_ids = jnp.arange(experts, dtype=jnp.int32)
    onehot = (routes[:, :, None] == expert_ids[None, None, :]).astype(jnp.float32)
    hit = jnp.sum(onehot, axis=1)
    priority = slot_order[0]
    before = (priority[None, :] < priority[:, None]).astype(jnp.float32)
    rank = jnp.dot(before, hit, precision=lax.Precision.HIGHEST)
    counts = jnp.sum(hit, axis=0)
    every = lax.all_gather(counts, ("rep", "ep")).reshape(groups, experts, experts)
    here = lax.dynamic_index_in_dim(every, rep_index, 0, keepdims=False)
    pair = jnp.bitwise_xor(rep_index, 1) % groups
    there = lax.dynamic_index_in_dim(every, pair, 0, keepdims=False)
    earlier = (jnp.arange(experts) < ep_index).astype(jnp.float32)
    start = jnp.sum(here * earlier[:, None], axis=0)
    load_there = jnp.sum(there, axis=0)
    caps = capacity.astype(jnp.float32)
    cap_here = lax.dynamic_index_in_dim(caps, rep_index, 0, keepdims=False)
    cap_there = lax.dynamic_index_in_dim(caps, pair, 0, keepdims=False)
    limit = cap_here + jnp.minimum(jnp.maximum(cap_there - load_there, 0.0), SPILL)
    kept_hit = hit * (start[None, :] + rank < limit[None, :]).astype(jnp.float32)
    return onehot, hit, rank, counts, kept_hit


def expert_rows(inputs, w_gate, w_up, w_down):
    gate_proj = jnp.dot(inputs, w_gate, preferred_element_type=jnp.float32)
    up_proj = jnp.dot(inputs, w_up, preferred_element_type=jnp.float32)
    hidden = (jax.nn.silu(gate_proj) * up_proj).astype(jnp.bfloat16)
    return jnp.dot(hidden, w_down, preferred_element_type=jnp.float32).astype(jnp.bfloat16)


def on_device(tokens, routes, gate_scores, slot_order, capacity, w_gate, w_up, w_down):
    experts = lax.axis_size("ep")
    tok_rows, width = tokens.shape
    onehot, hit, rank, counts, kept_hit = routing(routes, slot_order, capacity)
    slot_ids = jnp.arange(SLOT, dtype=jnp.float32)
    slot_match = hit[:, :, None] * (rank[:, :, None] == slot_ids[None, None, :]).astype(jnp.float32)
    token_ids = jnp.arange(tok_rows, dtype=jnp.float32)
    select = slot_match.reshape(tok_rows, experts * SLOT).astype(jnp.bfloat16)
    outgoing = lax.dot_general(
        select, tokens, (((0,), (0,)), ((), ())), preferred_element_type=jnp.float32
    ).astype(jnp.bfloat16)
    outgoing = outgoing.reshape(experts, SLOT, width)
    arrived = lax.all_to_all(outgoing, "ep", split_axis=0, concat_axis=0, tiled=True)
    results = expert_rows(arrived.reshape(experts * SLOT, width), w_gate[0], w_up[0], w_down[0])
    returned = lax.all_to_all(
        results.reshape(experts, SLOT, width), "ep", split_axis=0, concat_axis=0, tiled=True
    )
    kept_mask = jnp.sum(onehot * kept_hit[:, None, :], axis=2)
    rank_pick = jnp.sum(onehot * rank[:, None, :], axis=2).astype(jnp.int32)
    row_index = routes * SLOT + rank_pick
    picked = returned.reshape(experts * SLOT, width)[row_index]
    gate_total = jnp.sum(gate_scores, axis=1)
    kept_sum = jnp.sum(gate_scores * kept_mask, axis=1)
    weight = gate_scores * kept_mask / jnp.maximum(kept_sum, 0.25 * gate_total)[:, None]
    mixed = jnp.sum(weight[:, :, None] * picked.astype(jnp.float32), axis=1)
    return mixed.astype(jnp.bfloat16)


def solution(mesh):
    placed = (
        P(("rep", "ep"), None),
        P(("rep", "ep"), None),
        P(("rep", "ep"), None),
        P(("rep", "ep"), None),
        P(),
        P("ep", None, None),
        P("ep", None, None),
        P("ep", None, None),
    )
    return jax.shard_map(
        on_device, mesh=mesh, in_specs=placed, out_specs=P(("rep", "ep"), None), check_vma=False
    )
```

```python
import functools

import jax
import jax.numpy as jnp
from jax import lax
from jax.experimental import pallas as pl
from jax.experimental.pallas import tpu as pltpu
from jax.sharding import PartitionSpec as P

SPILL = 768.0
SIDE = 4
CHUNKS = 2
MESH = pl.DeviceIdType.MESH


def routing_weights(routes, gate_scores, slot_order, capacity):
    experts = lax.axis_size("ep")
    groups = lax.axis_size("rep")
    ep_index = lax.axis_index("ep")
    rep_index = lax.axis_index("rep")
    expert_ids = jnp.arange(experts, dtype=jnp.int32)
    onehot = (routes[:, :, None] == expert_ids[None, None, :]).astype(jnp.float32)
    hit = jnp.sum(onehot, axis=1)
    score = jnp.sum(onehot * gate_scores[:, :, None], axis=1)
    priority = slot_order[0]
    before = (priority[None, :] < priority[:, None]).astype(jnp.bfloat16)
    rank = jnp.dot(before, hit.astype(jnp.bfloat16), preferred_element_type=jnp.float32)
    counts = jnp.sum(hit, axis=0)
    every = lax.all_to_all(
        jnp.broadcast_to(counts[None, :], (experts, experts)), "ep", 0, 0, tiled=True
    )
    load = jnp.sum(every, axis=0)
    pairs = [(i, (i ^ 1) % groups) for i in range(groups)]
    load_there = lax.ppermute(load, "rep", pairs)
    earlier = (jnp.arange(experts) < ep_index).astype(jnp.float32)
    start = jnp.sum(every * earlier[:, None], axis=0)
    caps = capacity.astype(jnp.float32)
    pair = jnp.bitwise_xor(rep_index, 1) % groups
    cap_here = lax.dynamic_index_in_dim(caps, rep_index, 0, keepdims=False)
    cap_there = lax.dynamic_index_in_dim(caps, pair, 0, keepdims=False)
    limit = cap_here + jnp.minimum(jnp.maximum(cap_there - load_there, 0.0), SPILL)
    kept = hit * (start[None, :] + rank < limit[None, :]).astype(jnp.float32)
    kept_score = score * kept
    total = jnp.sum(gate_scores, axis=1)
    kept_sum = jnp.sum(kept_score, axis=1)
    weight = kept_score / jnp.maximum(kept_sum, 0.25 * total)[:, None]
    return weight.T


def spread_weights(weight_t, rows):
    experts = lax.axis_size("ep")
    me = lax.axis_index("ep")
    core, col, row = me % 2, (me // 2) % SIDE, me // (2 * SIDE)
    tok_rows = weight_t.shape[1]
    swapped = weight_t.reshape(experts // 2, 2, tok_rows)[:, ::-1].reshape(experts, tok_rows)
    sent = jnp.stack([weight_t, swapped], axis=1)
    got = lax.all_to_all(sent, "ep", 0, 0, tiled=True)
    got = got.reshape(SIDE, SIDE, 2, 2, tok_rows)
    mine = lax.dynamic_index_in_dim(got, core, 2, keepdims=False)
    mine = lax.dynamic_slice_in_dim(jnp.concatenate([mine, mine], 0), row, SIDE, 0)
    mine = lax.dynamic_slice_in_dim(jnp.concatenate([mine, mine], 1), col, SIDE, 1)
    mine = mine.reshape(SIDE, SIDE, 2, CHUNKS, 2, rows)
    first = mine[:, :, :, :, 0].transpose(3, 0, 1, 4, 2)
    second = mine[:, :, :, :, 1].transpose(3, 1, 0, 4, 2)
    both = jnp.stack([first, second], axis=2)
    return both.reshape(CHUNKS * SIDE, 2 * SIDE * rows, 2)


def kernel(
    tok, wt, wg, wu, wd,
    out, xg, rh, rf,
    wgv, wuv, wdv, xv, stg, total, hid, rv, st2, ph, pf,
    load_sem, own_sem, send_sem, recv_sem,
):
    me = lax.axis_index("ep")
    core, col, row = me % 2, (me // 2) % SIDE, me // (2 * SIDE)

    def at(r, c, k):
        return (r * SIDE + c) * 2 + k

    x_next, x_prev = at(row, (col + 1) % SIDE, core), at(row, (col + 3) % SIDE, core)
    z_next, z_prev = at((row + 1) % SIDE, col, core), at((row + 3) % SIDE, col, core)
    twin = at(row, col, 1 - core)
    near = ((x_next, x_prev), (z_next, z_prev))
    far = ((z_next, z_prev), (x_next, x_prev))

    depth = tok.shape[1]
    inner = wg.shape[1]
    rows = tok.shape[0] // (2 * CHUNKS)
    half = rows // 2
    group = SIDE * rows
    ghalf = group // 2
    ntile = min(256, inner)
    otile = min(512, depth)

    barrier = pltpu.get_barrier_semaphore()
    for dev in (x_next, x_prev, z_next, z_prev, twin):
        pl.semaphore_signal(barrier, inc=1, device_id={"ep": dev}, device_id_type=MESH)

    made = []

    def send(src, dst, dev):
        k = len(made)
        copy = pltpu.make_async_remote_copy(
            src_ref=src, dst_ref=dst, send_sem=send_sem.at[k], recv_sem=recv_sem.at[k],
            device_id={"ep": dev}, device_id_type=MESH,
        )
        copy.start()
        made.append(copy)
        return copy

    stage_in = pltpu.make_async_copy(tok, xv.at[pl.ds(0, tok.shape[0])], load_sem.at[0])
    stage_in.start()
    pl.semaphore_wait(barrier, 5)

    own = {}

    def start_own(c):
        for r in range(2):
            src = tok.at[pl.ds((2 * c + r) * rows, rows)]
            own[c, r, 0] = send(src, xg.at[c, r, 0, pl.ds(3 * rows, rows)], near[r][0])
            own[c, r, 1] = send(src, xg.at[c, r, 0, pl.ds(rows, rows)], near[r][1])

    relay = {}

    def start_relay(c):
        for r in range(2):
            own[c, r, 1].wait_recv()
            relay[c, r, 1] = send(
                xg.at[c, r, 0, pl.ds(rows, half)],
                xg.at[c, r, 0, pl.ds(2 * rows, half)], near[r][1],
            )
            own[c, r, 0].wait_recv()
            relay[c, r, 0] = send(
                xg.at[c, r, 0, pl.ds(3 * rows + half, half)],
                xg.at[c, r, 0, pl.ds(2 * rows + half, half)], near[r][0],
            )

    wide = {}

    def start_wide(c):
        for r in range(2):
            relay[c, r, 0].wait_recv()
            relay[c, r, 1].wait_recv()
        for part in range(2):
            for r in range(2):
                lo = pl.ds(part * ghalf, ghalf)
                hi = pl.ds((1 - part) * ghalf, ghalf)
                wide[c, r, 1, part] = send(xg.at[c, r, 0, lo], xg.at[c, r, 1, lo], far[r][1])
                wide[c, r, 0, part] = send(xg.at[c, r, 0, hi], xg.at[c, r, 3, hi], far[r][0])

    last = {}

    def start_last(c):
        for r in range(2):
            lo = pl.ds(0, ghalf)
            hi = pl.ds(ghalf, ghalf)
            wide[c, r, 1, 0].wait_recv()
            last[c, r, 1] = send(xg.at[c, r, 1, lo], xg.at[c, r, 2, lo], far[r][1])
            wide[c, r, 0, 0].wait_recv()
            last[c, r, 0] = send(xg.at[c, r, 3, hi], xg.at[c, r, 2, hi], far[r][0])

    def end_gather(c):
        for r in range(2):
            for k in range(2):
                wide[c, r, k, 1].wait_recv()
                last[c, r, k].wait_recv()

    start_own(0)
    weights = []
    for k, (src, dst) in enumerate(
        ((wg, wgv.at[:, pl.ds(0, inner)]), (wu, wuv.at[:, pl.ds(0, inner)]), (wd, wdv.at[pl.ds(0, inner)]))
    ):
        copy = pltpu.make_async_copy(src, dst, own_sem.at[k])
        copy.start()
        weights.append(copy)
    swaps = [
        send(wg, wgv.at[:, pl.ds(inner, inner)], twin),
        send(wu, wuv.at[:, pl.ds(inner, inner)], twin),
        send(wd, wdv.at[pl.ds(inner, inner)], twin),
    ]
    stage_in.wait()
    stage_out = []
    for c in range(CHUNKS):
        for r in range(2):
            copy = pltpu.make_async_copy(
                xv.at[pl.ds((2 * c + r) * rows, rows)],
                xg.at[c, r, 0, pl.ds(0, rows)], own_sem.at[3 + 2 * c + r],
            )
            copy.start()
            stage_out.append(copy)
    start_relay(0)
    start_own(1)
    for copy in stage_out:
        copy.wait()
    start_wide(0)
    start_relay(1)
    start_last(0)
    start_wide(1)
    for copy in weights:
        copy.wait()
    for copy in swaps:
        copy.wait_recv()
    end_gather(0)

    def fetch(c, d):
        copies = []
        for r in range(2):
            copy = pltpu.make_async_copy(
                xg.at[c, r, d], xv.at[pl.ds(r * group, group)], load_sem.at[r]
            )
            copy.start()
            copies.append(copy)
        return copies

    def up_phase(c, d):
        index = c * SIDE + d
        for e in range(2):
            scale = wt[index, :, e:e + 1]

            def tile(n, carry):
                cols = pl.ds(pl.multiple_of(e * inner + n * ntile, ntile), ntile)
                gate = jnp.dot(xv[...], wgv[:, cols], preferred_element_type=jnp.float32)
                up = jnp.dot(xv[...], wuv[:, cols], preferred_element_type=jnp.float32)
                hidden = gate / (1.0 + jnp.exp(-gate)) * up * scale
                hid[:, cols] = hidden.astype(jnp.bfloat16)
                return carry

            lax.fori_loop(0, inner // ntile, tile, 0)

    def down_phase(finish):
        def tile(n, carry):
            cols = pl.ds(pl.multiple_of(n * otile, otile), otile)
            finish(cols, jnp.dot(hid[...], wdv[:, cols], preferred_element_type=jnp.float32))
            return carry

        lax.fori_loop(0, depth // otile, tile, 0)

    def bring(pieces):
        copies = []
        for k, (src, dst) in enumerate(pieces):
            copy = pltpu.make_async_copy(src, dst, load_sem.at[2 + k])
            copy.start()
            copies.append(copy)
        for copy in copies:
            copy.wait()

    halves, fulls, near_h, near_f = {}, {}, {}, {}

    def reuse(sent, c, keys):
        if c > 0:
            for key in keys:
                sent[(c - 1,) + key].wait_send()

    def finish_two(c):
        reuse(halves, c, [(r, k) for r in range(2) for k in range(2)])

        def store(cols, part):
            stg[0, :, cols] = part.astype(jnp.bfloat16)

        down_phase(store)
        for r in range(2):
            halves[c, r, 0] = send(stg.at[0, pl.ds(r * group, ghalf)], rh.at[c, 0, r], far[r][0])
            halves[c, r, 1] = send(stg.at[0, pl.ds(r * group + ghalf, ghalf)], rh.at[c, 1, r], far[r][1])

    def finish_side(c, k):
        for r in range(2):
            halves[c, r, k].wait_recv()
        bring([(rh.at[c, k, r], rv.at[0, pl.ds(r * ghalf, ghalf)]) for r in range(2)])
        reuse(fulls, c, [(r, k) for r in range(2)])

        def store(cols, part):
            for r in range(2):
                with_it = r * group + k * ghalf
                alone = r * group + (1 - k) * ghalf
                added = part[with_it:with_it + ghalf] + rv[0, pl.ds(r * ghalf, ghalf), cols].astype(jnp.float32)
                stg[1 + k, pl.ds(with_it, ghalf), cols] = added.astype(jnp.bfloat16)
                stg[1 + k, pl.ds(alone, ghalf), cols] = part[alone:alone + ghalf].astype(jnp.bfloat16)

        down_phase(store)
        for r in range(2):
            fulls[c, r, k] = send(stg.at[1 + k, pl.ds(r * group, group)], rf.at[c, k, r], far[r][k])

    def finish_own(c):
        pieces = []
        for k in range(2):
            for r in range(2):
                fulls[c, r, k].wait_recv()
                pieces.append((rf.at[c, k, r], rv.at[k, pl.ds(r * group, group)]))
        bring(pieces)

        def store(cols, part):
            total[:, cols] = (
                part + rv[0, :, cols].astype(jnp.float32) + rv[1, :, cols].astype(jnp.float32)
            )

        down_phase(store)

    def near_start(c):
        reuse(near_h, c, [(r, k) for r in range(2) for k in range(2)])
        for r in range(2):
            st2[0, pl.ds(r * rows, rows)] = total[pl.ds(r * group + 2 * rows, rows)].astype(jnp.bfloat16)
        for r in range(2):
            near_h[c, r, 0] = send(st2.at[0, pl.ds(r * rows, half)], ph.at[c, 0, r], near[r][0])
            near_h[c, r, 1] = send(st2.at[0, pl.ds(r * rows + half, half)], ph.at[c, 1, r], near[r][1])

    def near_middle(c):
        reuse(near_f, c, [(r, k) for r in range(2) for k in range(2)])
        for k in range(2):
            for r in range(2):
                near_h[c, r, k].wait_recv()
                base = r * group + (1 + 2 * k) * rows
                with_it, alone = k * half, (1 - k) * half
                st2[1 + k, pl.ds(r * rows + with_it, half)] = (
                    total[pl.ds(base + with_it, half)] + ph[c, k, r].astype(jnp.float32)
                ).astype(jnp.bfloat16)
                st2[1 + k, pl.ds(r * rows + alone, half)] = total[pl.ds(base + alone, half)].astype(jnp.bfloat16)
                near_f[c, r, k] = send(st2.at[1 + k, pl.ds(r * rows, rows)], pf.at[c, k, r], near[r][k])

    def near_end(c):
        for r in range(2):
            for k in range(2):
                near_f[c, r, k].wait_recv()
            out[pl.ds((2 * c + r) * rows, rows)] = (
                total[pl.ds(r * group, rows)]
                + pf[c, 0, r].astype(jnp.float32)
                + pf[c, 1, r].astype(jnp.float32)
            ).astype(jnp.bfloat16)

    order = (2, 1, 3, 0)
    waiting = fetch(0, 2)
    for c in range(CHUNKS):
        for place, d in enumerate(order):
            for copy in waiting:
                copy.wait()
            up_phase(c, d)
            if c == 0 and place == 0:
                start_last(1)
            if place < 3:
                waiting = fetch(c, order[place + 1])
            elif c + 1 < CHUNKS:
                end_gather(c + 1)
                waiting = fetch(c + 1, order[0])
            if d == 2:
                finish_two(c)
                if c > 0:
                    near_middle(c - 1)
            elif d == 0:
                finish_own(c)
            else:
                finish_side(c, 0 if d == 1 else 1)
                if c > 0 and d == 1:
                    near_end(c - 1)
        near_start(c)
    near_middle(CHUNKS - 1)
    near_end(CHUNKS - 1)

    waited = set()
    for sent in (halves, fulls, near_h, near_f):
        for key, copy in sent.items():
            if key[0] < CHUNKS - 1:
                waited.add(id(copy))
    for copy in made:
        if id(copy) not in waited:
            copy.wait_send()


N_MESSAGES = CHUNKS * 36 + 3


def expert_layer(tokens, weights, w_gate, w_up, w_down):
    tok_rows, depth = tokens.shape
    inner = w_gate.shape[1]
    rows = tok_rows // (2 * CHUNKS)
    group = SIDE * rows
    unit = 2 * group
    bf16 = jnp.bfloat16
    hbm = pl.BlockSpec(memory_space=pl.ANY)
    vmem = pl.BlockSpec(memory_space=pltpu.VMEM)
    shapes = (
        jax.ShapeDtypeStruct((tok_rows, depth), bf16),
        jax.ShapeDtypeStruct((CHUNKS, 2, SIDE, group, depth), bf16),
        jax.ShapeDtypeStruct((CHUNKS, 2, 2, group // 2, depth), bf16),
        jax.ShapeDtypeStruct((CHUNKS, 2, 2, group, depth), bf16),
    )
    scratch = [
        pltpu.VMEM((depth, 2 * inner), bf16),
        pltpu.VMEM((depth, 2 * inner), bf16),
        pltpu.VMEM((2 * inner, depth), bf16),
        pltpu.VMEM((unit, depth), bf16),
        pltpu.VMEM((3, unit, depth), bf16),
        pltpu.VMEM((unit, depth), jnp.float32),
        pltpu.VMEM((unit, 2 * inner), bf16),
        pltpu.VMEM((2, unit, depth), bf16),
        pltpu.VMEM((3, 2 * rows, depth), bf16),
        pltpu.VMEM((CHUNKS, 2, 2, rows // 2, depth), bf16),
        pltpu.VMEM((CHUNKS, 2, 2, rows, depth), bf16),
        pltpu.SemaphoreType.DMA((6,)),
        pltpu.SemaphoreType.DMA((3 + 2 * CHUNKS,)),
        pltpu.SemaphoreType.DMA((N_MESSAGES,)),
        pltpu.SemaphoreType.DMA((N_MESSAGES,)),
    ]
    return pl.pallas_call(
        kernel,
        out_shape=shapes,
        in_specs=[hbm, vmem, hbm, hbm, hbm],
        out_specs=(vmem, hbm, hbm, hbm),
        scratch_shapes=scratch,
        compiler_params=pltpu.CompilerParams(
            collective_id=0, has_side_effects=True, vmem_limit_bytes=66 * 1000 * 1000
        ),
    )(tokens, weights, w_gate, w_up, w_down)[0]


def on_device(tokens, routes, gate_scores, slot_order, capacity, w_gate, w_up, w_down):
    weight_t = routing_weights(routes, gate_scores, slot_order, capacity)
    spread = spread_weights(weight_t, tokens.shape[0] // (2 * CHUNKS))
    return expert_layer(tokens, spread, w_gate[0], w_up[0], w_down[0])


def solution(mesh):
    placed = (
        P(("rep", "ep"), None),
        P(("rep", "ep"), None),
        P(("rep", "ep"), None),
        P(("rep", "ep"), None),
        P(),
        P("ep", None, None),
        P("ep", None, None),
        P("ep", None, None),
    )
    return jax.shard_map(
        on_device, mesh=mesh, in_specs=placed, out_specs=P(("rep", "ep"), None), check_vma=False
    )
```

```python
import functools

import jax
import jax.numpy as jnp
from jax import lax
from jax.experimental import pallas as pl
from jax.experimental.pallas import tpu as pltpu
from jax.sharding import PartitionSpec as P

SPILL = 768.0
SIDE = 4
CHUNKS = 2
MESH = pl.DeviceIdType.MESH


def routing_weights(routes, gate_scores, slot_order, capacity):
    experts = lax.axis_size("ep")
    groups = lax.axis_size("rep")
    ep_index = lax.axis_index("ep")
    rep_index = lax.axis_index("rep")
    expert_ids = jnp.arange(experts, dtype=jnp.int32)
    onehot = (routes[:, :, None] == expert_ids[None, None, :]).astype(jnp.float32)
    hit = jnp.sum(onehot, axis=1)
    score = jnp.sum(onehot * gate_scores[:, :, None], axis=1)
    priority = slot_order[0]
    before = (priority[None, :] < priority[:, None]).astype(jnp.bfloat16)
    rank = jnp.dot(before, hit.astype(jnp.bfloat16), preferred_element_type=jnp.float32)
    counts = jnp.sum(hit, axis=0)
    every = lax.all_to_all(
        jnp.broadcast_to(counts[None, :], (experts, experts)), "ep", 0, 0, tiled=True
    )
    load = jnp.sum(every, axis=0)
    pairs = [(i, (i ^ 1) % groups) for i in range(groups)]
    load_there = lax.ppermute(load, "rep", pairs)
    earlier = (jnp.arange(experts) < ep_index).astype(jnp.float32)
    start = jnp.sum(every * earlier[:, None], axis=0)
    caps = capacity.astype(jnp.float32)
    pair = jnp.bitwise_xor(rep_index, 1) % groups
    cap_here = lax.dynamic_index_in_dim(caps, rep_index, 0, keepdims=False)
    cap_there = lax.dynamic_index_in_dim(caps, pair, 0, keepdims=False)
    limit = cap_here + jnp.minimum(jnp.maximum(cap_there - load_there, 0.0), SPILL)
    kept = hit * (start[None, :] + rank < limit[None, :]).astype(jnp.float32)
    kept_score = score * kept
    total = jnp.sum(gate_scores, axis=1)
    kept_sum = jnp.sum(kept_score, axis=1)
    weight = kept_score / jnp.maximum(kept_sum, 0.25 * total)[:, None]
    return weight.T


def spread_weights(weight_t, rows):
    experts = lax.axis_size("ep")
    me = lax.axis_index("ep")
    core, col, row = me % 2, (me // 2) % SIDE, me // (2 * SIDE)
    tok_rows = weight_t.shape[1]
    swapped = weight_t.reshape(experts // 2, 2, tok_rows)[:, ::-1].reshape(experts, tok_rows)
    sent = jnp.stack([weight_t, swapped], axis=1)
    got = lax.all_to_all(sent, "ep", 0, 0, tiled=True)
    got = got.reshape(SIDE, SIDE, 2, 2, tok_rows)
    mine = lax.dynamic_index_in_dim(got, core, 2, keepdims=False)
    mine = lax.dynamic_slice_in_dim(jnp.concatenate([mine, mine], 0), row, SIDE, 0)
    mine = lax.dynamic_slice_in_dim(jnp.concatenate([mine, mine], 1), col, SIDE, 1)
    mine = mine.reshape(SIDE, SIDE, 2, CHUNKS, 2, rows)
    first = mine[:, :, :, :, 0].transpose(3, 0, 1, 4, 2)
    second = mine[:, :, :, :, 1].transpose(3, 1, 0, 4, 2)
    both = jnp.stack([first, second], axis=2)
    return both.reshape(CHUNKS * SIDE, 2 * SIDE * rows, 2)


def kernel(
    tok, wt, wg, wu, wd,
    out, xg, rh, rf, part,
    wgv, wuv, wdv, xv, stg, mix, total, hid, rv, st2, ph, pf,
    load_sem, own_sem, put_sem, send_sem, recv_sem,
):
    me = lax.axis_index("ep")
    core, col, row = me % 2, (me // 2) % SIDE, me // (2 * SIDE)

    def at(r, c, k):
        return (r * SIDE + c) * 2 + k

    x_next, x_prev = at(row, (col + 1) % SIDE, core), at(row, (col + 3) % SIDE, core)
    z_next, z_prev = at((row + 1) % SIDE, col, core), at((row + 3) % SIDE, col, core)
    twin = at(row, col, 1 - core)
    near = ((x_next, x_prev), (z_next, z_prev))
    far = ((z_next, z_prev), (x_next, x_prev))

    depth = tok.shape[1]
    inner = wg.shape[1]
    rows = tok.shape[0] // (2 * CHUNKS)
    half = rows // 2
    group = SIDE * rows
    ghalf = group // 2
    ntile = min(256, inner)
    otile = min(512, depth)

    barrier = pltpu.get_barrier_semaphore()
    for dev in (x_next, x_prev, z_next, z_prev, twin):
        pl.semaphore_signal(barrier, inc=1, device_id={"ep": dev}, device_id_type=MESH)

    made = []

    def send(src, dst, dev):
        k = len(made)
        copy = pltpu.make_async_remote_copy(
            src_ref=src, dst_ref=dst, send_sem=send_sem.at[k], recv_sem=recv_sem.at[k],
            device_id={"ep": dev}, device_id_type=MESH,
        )
        copy.start()
        made.append(copy)
        return copy

    stage_in = pltpu.make_async_copy(tok, xv.at[pl.ds(0, tok.shape[0])], load_sem.at[0])
    stage_in.start()
    pl.semaphore_wait(barrier, 5)

    own = {}

    def start_own(c):
        for r in range(2):
            src = tok.at[pl.ds((2 * c + r) * rows, rows)]
            own[c, r, 0] = send(src, xg.at[c, r, 0, pl.ds(3 * rows, rows)], near[r][0])
            own[c, r, 1] = send(src, xg.at[c, r, 0, pl.ds(rows, rows)], near[r][1])

    relay = {}

    def start_relay(c):
        for r in range(2):
            own[c, r, 1].wait_recv()
            relay[c, r, 1] = send(
                xg.at[c, r, 0, pl.ds(rows, half)],
                xg.at[c, r, 0, pl.ds(2 * rows, half)], near[r][1],
            )
            own[c, r, 0].wait_recv()
            relay[c, r, 0] = send(
                xg.at[c, r, 0, pl.ds(3 * rows + half, half)],
                xg.at[c, r, 0, pl.ds(2 * rows + half, half)], near[r][0],
            )

    wide = {}

    def start_wide(c):
        for r in range(2):
            relay[c, r, 0].wait_recv()
            relay[c, r, 1].wait_recv()
        for part in range(2):
            for r in range(2):
                lo = pl.ds(part * ghalf, ghalf)
                hi = pl.ds((1 - part) * ghalf, ghalf)
                wide[c, r, 1, part] = send(xg.at[c, r, 0, lo], xg.at[c, r, 1, lo], far[r][1])
                wide[c, r, 0, part] = send(xg.at[c, r, 0, hi], xg.at[c, r, 3, hi], far[r][0])

    last = {}

    def start_last(c):
        for r in range(2):
            lo = pl.ds(0, ghalf)
            hi = pl.ds(ghalf, ghalf)
            wide[c, r, 1, 0].wait_recv()
            last[c, r, 1] = send(xg.at[c, r, 1, lo], xg.at[c, r, 2, lo], far[r][1])
            wide[c, r, 0, 0].wait_recv()
            last[c, r, 0] = send(xg.at[c, r, 3, hi], xg.at[c, r, 2, hi], far[r][0])

    def end_gather(c):
        for r in range(2):
            for k in range(2):
                wide[c, r, k, 1].wait_recv()
                last[c, r, k].wait_recv()

    start_own(0)
    weights = []
    for k, (src, dst) in enumerate(
        ((wg, wgv.at[:, pl.ds(0, inner)]), (wu, wuv.at[:, pl.ds(0, inner)]), (wd, wdv.at[pl.ds(0, inner)]))
    ):
        copy = pltpu.make_async_copy(src, dst, own_sem.at[k])
        copy.start()
        weights.append(copy)
    swaps = [
        send(wg, wgv.at[:, pl.ds(inner, inner)], twin),
        send(wu, wuv.at[:, pl.ds(inner, inner)], twin),
        send(wd, wdv.at[pl.ds(inner, inner)], twin),
    ]
    stage_in.wait()
    stage_out = []
    for c in range(CHUNKS):
        for r in range(2):
            copy = pltpu.make_async_copy(
                xv.at[pl.ds((2 * c + r) * rows, rows)],
                xg.at[c, r, 0, pl.ds(0, rows)], own_sem.at[3 + 2 * c + r],
            )
            copy.start()
            stage_out.append(copy)
    start_relay(0)
    start_own(1)
    for copy in stage_out:
        copy.wait()
    start_wide(0)
    start_relay(1)
    start_last(0)
    start_wide(1)
    for copy in weights:
        copy.wait()
    for copy in swaps:
        copy.wait_recv()
    end_gather(0)

    def fetch(c, d):
        copies = []
        for r in range(2):
            copy = pltpu.make_async_copy(
                xg.at[c, r, d], xv.at[pl.ds(r * group, group)], load_sem.at[r]
            )
            copy.start()
            copies.append(copy)
        return copies

    def up_phase(c, d):
        index = c * SIDE + d
        for e in range(2):
            scale = wt[index, :, e:e + 1]

            def tile(n, carry):
                cols = pl.ds(pl.multiple_of(e * inner + n * ntile, ntile), ntile)
                gate = jnp.dot(xv[...], wgv[:, cols], preferred_element_type=jnp.float32)
                up = jnp.dot(xv[...], wuv[:, cols], preferred_element_type=jnp.float32)
                hidden = gate / (1.0 + jnp.exp(-gate)) * up * scale
                hid[:, cols] = hidden.astype(jnp.bfloat16)
                return carry

            lax.fori_loop(0, inner // ntile, tile, 0)

    def down_phase(c, d, slot):
        def put(n):
            cols = pl.ds(pl.multiple_of(n * otile, otile), otile)
            pltpu.make_async_copy(
                stg.at[slot, :, cols], part.at[c, d, :, cols], put_sem.at[slot]
            ).start()

        def tile(n, carry):
            cols = pl.ds(pl.multiple_of(n * otile, otile), otile)
            value = jnp.dot(hid[...], wdv[:, cols], preferred_element_type=jnp.float32)
            stg[slot, :, cols] = value.astype(jnp.bfloat16)

            @pl.when(n > 0)
            def _():
                put(n - 1)

            return carry

        lax.fori_loop(0, depth // otile, tile, 0)
        put(depth // otile - 1)
        pltpu.make_async_copy(stg.at[slot], part.at[c, d], put_sem.at[slot]).wait()

    def bring(pieces):
        copies = []
        for k, (src, dst) in enumerate(pieces):
            copy = pltpu.make_async_copy(src, dst, load_sem.at[2 + k])
            copy.start()
            copies.append(copy)
        for copy in copies:
            copy.wait()

    halves, alones, fulls, near_h, near_f = {}, {}, {}, {}, {}

    def reuse(sent, c, keys):
        if c > 0:
            for key in keys:
                sent[(c - 1,) + key].wait_send()

    def far_halves(c):
        for r in range(2):
            halves[c, r, 0] = send(part.at[c, 2, pl.ds(r * group, ghalf)], rh.at[c, 0, r], far[r][0])
            halves[c, r, 1] = send(part.at[c, 2, pl.ds(r * group + ghalf, ghalf)], rh.at[c, 1, r], far[r][1])

    def far_alone(c, k):
        for r in range(2):
            alone = (1 - k) * ghalf
            src = part.at[c, 1 + 2 * k, pl.ds(r * group + alone, ghalf)]
            alones[c, r, k] = send(src, rf.at[c, k, r, pl.ds(alone, ghalf)], far[r][k])

    def far_sum(c):
        reuse(fulls, c, [(r, k) for r in range(2) for k in range(2)])
        pieces = []
        for k in range(2):
            for r in range(2):
                halves[c, r, k].wait_recv()
                to = pl.ds((2 * k + r) * ghalf, ghalf)
                pieces.append((rh.at[c, k, r], rv.at[0, to]))
                pieces.append((part.at[c, 1 + 2 * k, pl.ds(r * group + k * ghalf, ghalf)], rv.at[1, to]))
        bring(pieces)

        def tile(n, carry):
            cols = pl.ds(pl.multiple_of(n * otile, otile), otile)
            added = rv[0, :, cols].astype(jnp.float32) + rv[1, :, cols].astype(jnp.float32)
            mix[:, cols] = added.astype(jnp.bfloat16)
            return carry

        lax.fori_loop(0, depth // otile, tile, 0)
        for k in range(2):
            for r in range(2):
                src = mix.at[pl.ds((2 * k + r) * ghalf, ghalf)]
                fulls[c, r, k] = send(src, rf.at[c, k, r, pl.ds(k * ghalf, ghalf)], far[r][k])

    def own_sum(c):
        pieces = [(part.at[c, 0], stg.at[0])]
        for k in range(2):
            for r in range(2):
                alones[c, r, k].wait_recv()
                fulls[c, r, k].wait_recv()
                pieces.append((rf.at[c, k, r], rv.at[k, pl.ds(r * group, group)]))
        bring(pieces)

        def tile(n, carry):
            cols = pl.ds(pl.multiple_of(n * otile, otile), otile)
            total[:, cols] = (
                stg[0, :, cols].astype(jnp.float32)
                + rv[0, :, cols].astype(jnp.float32)
                + rv[1, :, cols].astype(jnp.float32)
            )
            return carry

        lax.fori_loop(0, depth // otile, tile, 0)

    def near_start(c):
        reuse(near_h, c, [(r, k) for r in range(2) for k in range(2)])
        for r in range(2):
            st2[0, pl.ds(r * rows, rows)] = total[pl.ds(r * group + 2 * rows, rows)].astype(jnp.bfloat16)
        for r in range(2):
            near_h[c, r, 0] = send(st2.at[0, pl.ds(r * rows, half)], ph.at[c, 0, r], near[r][0])
            near_h[c, r, 1] = send(st2.at[0, pl.ds(r * rows + half, half)], ph.at[c, 1, r], near[r][1])

    def near_middle(c):
        reuse(near_f, c, [(r, k) for r in range(2) for k in range(2)])
        for k in range(2):
            for r in range(2):
                near_h[c, r, k].wait_recv()
                base = r * group + (1 + 2 * k) * rows
                with_it, alone = k * half, (1 - k) * half
                st2[1 + k, pl.ds(r * rows + with_it, half)] = (
                    total[pl.ds(base + with_it, half)] + ph[c, k, r].astype(jnp.float32)
                ).astype(jnp.bfloat16)
                st2[1 + k, pl.ds(r * rows + alone, half)] = total[pl.ds(base + alone, half)].astype(jnp.bfloat16)
                near_f[c, r, k] = send(st2.at[1 + k, pl.ds(r * rows, rows)], pf.at[c, k, r], near[r][k])

    def near_end(c):
        for r in range(2):
            for k in range(2):
                near_f[c, r, k].wait_recv()
            out[pl.ds((2 * c + r) * rows, rows)] = (
                total[pl.ds(r * group, rows)]
                + pf[c, 0, r].astype(jnp.float32)
                + pf[c, 1, r].astype(jnp.float32)
            ).astype(jnp.bfloat16)

    order = (2, 1, 3, 0)
    waiting = fetch(0, 2)
    for c in range(CHUNKS):
        for place, d in enumerate(order):
            for copy in waiting:
                copy.wait()
            up_phase(c, d)
            if c == 0 and place == 0:
                start_last(1)
            if place < 3:
                waiting = fetch(c, order[place + 1])
            elif c + 1 < CHUNKS:
                end_gather(c + 1)
                waiting = fetch(c + 1, order[0])
            down_phase(c, d, 1)
            if d == 2:
                far_halves(c)
            elif d == 1:
                far_alone(c, 0)
                if c > 0:
                    own_sum(c - 1)
                    near_start(c - 1)
            elif d == 3:
                far_alone(c, 1)
                if c > 0:
                    near_middle(c - 1)
                if c == CHUNKS - 1:
                    far_sum(c)
            elif c > 0:
                near_end(c - 1)
            else:
                far_sum(c)
    last_chunk = CHUNKS - 1
    own_sum(last_chunk)
    near_start(last_chunk)
    near_middle(last_chunk)
    near_end(last_chunk)

    waited = set()
    for sent in (fulls, near_h, near_f):
        for key, copy in sent.items():
            if key[0] < CHUNKS - 1:
                waited.add(id(copy))
    for copy in made:
        if id(copy) not in waited:
            copy.wait_send()


N_MESSAGES = CHUNKS * 40 + 3


def expert_layer(tokens, weights, w_gate, w_up, w_down):
    tok_rows, depth = tokens.shape
    inner = w_gate.shape[1]
    rows = tok_rows // (2 * CHUNKS)
    group = SIDE * rows
    unit = 2 * group
    bf16 = jnp.bfloat16
    hbm = pl.BlockSpec(memory_space=pl.ANY)
    vmem = pl.BlockSpec(memory_space=pltpu.VMEM)
    shapes = (
        jax.ShapeDtypeStruct((tok_rows, depth), bf16),
        jax.ShapeDtypeStruct((CHUNKS, 2, SIDE, group, depth), bf16),
        jax.ShapeDtypeStruct((CHUNKS, 2, 2, group // 2, depth), bf16),
        jax.ShapeDtypeStruct((CHUNKS, 2, 2, group, depth), bf16),
        jax.ShapeDtypeStruct((CHUNKS, SIDE, unit, depth), bf16),
    )
    scratch = [
        pltpu.VMEM((depth, 2 * inner), bf16),
        pltpu.VMEM((depth, 2 * inner), bf16),
        pltpu.VMEM((2 * inner, depth), bf16),
        pltpu.VMEM((unit, depth), bf16),
        pltpu.VMEM((2, unit, depth), bf16),
        pltpu.VMEM((unit, depth), bf16),
        pltpu.VMEM((unit, depth), jnp.float32),
        pltpu.VMEM((unit, 2 * inner), bf16),
        pltpu.VMEM((2, unit, depth), bf16),
        pltpu.VMEM((3, 2 * rows, depth), bf16),
        pltpu.VMEM((CHUNKS, 2, 2, rows // 2, depth), bf16),
        pltpu.VMEM((CHUNKS, 2, 2, rows, depth), bf16),
        pltpu.SemaphoreType.DMA((10,)),
        pltpu.SemaphoreType.DMA((3 + 2 * CHUNKS,)),
        pltpu.SemaphoreType.DMA((2,)),
        pltpu.SemaphoreType.DMA((N_MESSAGES,)),
        pltpu.SemaphoreType.DMA((N_MESSAGES,)),
    ]
    return pl.pallas_call(
        kernel,
        out_shape=shapes,
        in_specs=[hbm, vmem, hbm, hbm, hbm],
        out_specs=(vmem, hbm, hbm, hbm, hbm),
        scratch_shapes=scratch,
        compiler_params=pltpu.CompilerParams(
            collective_id=0, has_side_effects=True, vmem_limit_bytes=66 * 1000 * 1000
        ),
    )(tokens, weights, w_gate, w_up, w_down)[0]


def on_device(tokens, routes, gate_scores, slot_order, capacity, w_gate, w_up, w_down):
    weight_t = routing_weights(routes, gate_scores, slot_order, capacity)
    spread = spread_weights(weight_t, tokens.shape[0] // (2 * CHUNKS))
    return expert_layer(tokens, spread, w_gate[0], w_up[0], w_down[0])


def solution(mesh):
    placed = (
        P(("rep", "ep"), None),
        P(("rep", "ep"), None),
        P(("rep", "ep"), None),
        P(("rep", "ep"), None),
        P(),
        P("ep", None, None),
        P("ep", None, None),
        P("ep", None, None),
    )
    return jax.shard_map(
        on_device, mesh=mesh, in_specs=placed, out_specs=P(("rep", "ep"), None), check_vma=False
    )
```
